768 devices in a mesh: dp: 64 (over z_hi, y, core), mp: 12 (over z_lo, x).
Axes of the slice: x: 4, y: 8, z: 12 (z_hi: 4, z_lo: 3; z = z_hi * 3 + z_lo), core: 2. Of those that a mesh axis runs over, the one named last changes fastest.
Arguments:
- token_factors: bfloat16 [12, 131072, 128], P('mp', 'dp'), may hold values from -6 to 6
- example_ids: int32 [64, 2048], P('dp'), may hold values from 0 to 7, never falling along the last dimension, each value on 1 to 1024 neighbouring positions
- left_factor: bfloat16 [12, 64, 64], P('mp'), may hold values from -0.75 to 0.75
- right_factor: bfloat16 [12, 64, 64], P('mp'), may hold values from -0.75 to 0.75
- query_features: bfloat16 [6144, 49152], P('dp', 'mp'), may hold values from -0.21875 to 0.21875
Outputs:
- influence: float32 [6144, 512], P(('dp', 'mp'))
The draws below stay inside these ranges and needn't reach their ends.
Inputs may be any that keep to these rules, and one draw needn't show every extreme that they name: `example_ids`: each row is non-decreasing, and every example 0 to 7 has 1 to 1024 tokens in each block.
All inputs are finite; a program needn't handle non-finite values.
Results may differ from the reference program's by a relative error of at most 0.0029.
Values may be sent and summed in bfloat16 or wider, within the bound.
No kernel may reach another device: no remote copies, remote signals or barrier semaphores. Data moves between devices by JAX's collectives and lax.ppermute only.
A program may use at most 32 MiB of HBM per device.

```python
import math
import jax
import jax.numpy as jnp
import numpy as np
from jax import lax

R = 64
TOK_DEV = 2048
EX_DEV = 8
LAYERS = 12
BLOCKS = 64
TOKENS = 131072
TRAIN = 512
QUERIES = 6144
FEAT = 49152


def levels(stream_key, dims, pieces, smallest, high):
    factor_of = 1.0
    for dim, parts in pieces:
        draws = jax.random.uniform(jax.random.fold_in(jax.random.fold_in(stream_key, 6), dim), (parts,), jnp.float32, smallest / len(pieces), high / len(pieces))
        factor_of = factor_of * jnp.repeat(jnp.exp(draws), dims[dim] // parts).reshape((-1,) + (1,) * (len(dims) - 1 - dim))
    return factor_of


def profile(amount, total, reach, skew):
    portions = [(1 << 20) // math.isqrt(grade ** skew) + 1 for grade in range(2, amount + 1)]
    surplus, given = total - reach - (amount - 1), [1] * (amount - 1)
    while surplus > 0:
        movable = [i for i in range(amount - 1) if given[i] < reach]
        whole, remaining = sum([portions[i] for i in movable]), surplus
        for i in movable:
            more = min(reach - given[i], max(1, remaining * portions[i] // whole), surplus)
            given[i] = given[i] + more
            surplus = surplus - more
    return np.array([reach] + given)


def ragged_sizes(own_key, amount, total, bound, lean):
    if amount == 2:
        one = jax.random.randint(own_key, (), max(1, total - bound), min(bound, total - 1) + 1)
        return jnp.stack([one, total - one])
    tallies = jnp.asarray(profile(amount, total, bound, lean), jnp.int32)
    pairs = (amount - 1) // 2
    giver, sink = tallies[1:1 + 2 * pairs:2], tallies[2:2 + 2 * pairs:2]
    margin = jnp.minimum(giver - 1, bound - sink)
    moved = jax.random.randint(jax.random.fold_in(own_key, 1), (pairs,), 0, 1 << 20) % (margin + 1)
    tallies = tallies.at[1:1 + 2 * pairs:2].set(giver - moved).at[2:2 + 2 * pairs:2].set(sink + moved)
    return tallies[jax.random.permutation(jax.random.fold_in(own_key, 2), amount)]


def noise(key, shape, width, reach, cuts=(), kind=jnp.bfloat16):
    array = width * jax.random.normal(key, shape, jnp.float32)
    if cuts:
        array = array * levels(key, shape, cuts, -0.22, 0.18)
    return jnp.clip(array, -reach, reach).astype(kind)


def setup_inputs(seed: int = 0) -> dict:
    keys = jax.random.split(jax.random.key(seed), 6)
    return {
        "token_factors": noise(keys[0], (LAYERS, TOKENS, 2 * R), 1.0, 6.0, ((0, 12), (1, 64))),
        "example_ids": jax.vmap(lambda own: jnp.searchsorted(jnp.cumsum(ragged_sizes(own, EX_DEV, TOK_DEV, TOK_DEV // 2, 0)), jnp.arange(TOK_DEV), side="right"))(jax.random.split(keys[1], BLOCKS)).reshape((BLOCKS, TOK_DEV)).astype(jnp.int32),
        "left_factor": noise(keys[2], (LAYERS, R, R), R ** -0.5, 0.75, ((0, 12),)),
        "right_factor": noise(keys[3], (LAYERS, R, R), R ** -0.5, 0.75, ((0, 12),)),
        "query_features": noise(keys[4], (QUERIES, FEAT), (LAYERS * R) ** -0.5, 0.21875, ((0, 64), (1, 12))),
    }


def precondition(factors, labels, left, right):
    inputs = factors[:, :R].astype(jnp.float32)
    outputs = factors[:, R:].astype(jnp.float32)
    outer = outputs[:, :, None] * inputs[:, None, :]
    summed = jax.ops.segment_sum(outer, labels, num_segments=EX_DEV)
    counts = jax.ops.segment_sum(jnp.ones(labels.shape, jnp.float32), labels, num_segments=EX_DEV)
    gradient = summed / counts[:, None, None]
    precond = jnp.einsum("ac,ecd,db->eab", left.astype(jnp.float32), gradient, right.astype(jnp.float32), precision=lax.Precision.HIGHEST)
    return precond.reshape(EX_DEV, R * R)


def reference(token_factors, example_ids, left_factor, right_factor, query_features):
    def one_block(index):
        factors = lax.dynamic_slice_in_dim(token_factors, index * TOK_DEV, TOK_DEV, axis=1)
        labels = example_ids[index]

        def one_layer(item):
            return precondition(item[0], labels, item[1], item[2])

        per_layer = lax.map(one_layer, (factors, left_factor, right_factor))
        return jnp.transpose(per_layer, (1, 0, 2)).reshape(EX_DEV, LAYERS * R * R)

    features = lax.map(one_block, jnp.arange(BLOCKS, dtype=jnp.int32))
    features = features.reshape(TRAIN, LAYERS * R * R).astype(jnp.bfloat16)
    queries = query_features.reshape(QUERIES, LAYERS, R * R)
    trains = features.reshape(TRAIN, LAYERS, R * R)

    def add_layer(total, layer):
        query_part = lax.dynamic_index_in_dim(queries, layer, axis=1, keepdims=False)
        train_part = lax.dynamic_index_in_dim(trains, layer, axis=1, keepdims=False)
        return total + jnp.dot(query_part, train_part.T, preferred_element_type=jnp.float32), None

    total, unused = lax.scan(add_layer, jnp.zeros((QUERIES, TRAIN), jnp.float32), jnp.arange(LAYERS, dtype=jnp.int32))
    return total
```

```python
import jax
import jax.numpy as jnp
from jax import lax
from jax.sharding import PartitionSpec as P

EX_DEV = 8


def score_block(queries, train_block):
    return lax.dot_general(
        queries, train_block, (((1,), (1,)), ((), ())), preferred_element_type=jnp.float32
    )


def shards(token_factors, example_ids, left_factor, right_factor, query_features):
    proj_rank = left_factor.shape[1]
    tokens_here = token_factors.shape[1]
    examples = EX_DEV
    labels = example_ids[0]
    onehot = labels[:, None] == jnp.arange(examples, dtype=jnp.int32)[None, :]
    selector = onehot.astype(jnp.bfloat16)
    counts = jnp.sum(onehot.astype(jnp.float32), axis=0)
    inputs = token_factors[0, :, :proj_rank]
    outputs = token_factors[0, :, proj_rank:]
    masked = (selector[:, :, None] * inputs[:, None, :]).reshape(tokens_here, examples * proj_rank)
    summed = lax.dot_general(
        outputs, masked, (((0,), (0,)), ((), ())), preferred_element_type=jnp.float32
    )
    gradient = (
        summed.reshape(proj_rank, examples, proj_rank).transpose(1, 0, 2) / counts[:, None, None]
    )
    precond = jnp.einsum(
        "ac,ecd,db->eab",
        left_factor[0].astype(jnp.float32),
        gradient,
        right_factor[0].astype(jnp.float32),
        precision=lax.Precision.HIGHEST,
    )
    pieces = precond.reshape(examples, proj_rank * proj_rank)
    features = pieces.astype(jnp.bfloat16)
    gathered = lax.all_gather(features, "dp", axis=0, tiled=True)
    partial_value = score_block(query_features, gathered)
    members = lax.axis_size("mp")
    parts = partial_value.reshape(members, partial_value.shape[0] // members, -1)
    traded = lax.all_to_all(parts, "mp", 0, 0, tiled=False)
    return jnp.sum(traded, axis=0)


def solution(mesh):
    placed = (
        P("mp", "dp", None),
        P("dp", None),
        P("mp", None, None),
        P("mp", None, None),
        P("dp", "mp"),
    )
    return jax.shard_map(
        shards, mesh=mesh, in_specs=placed, out_specs=P(("dp", "mp"), None), check_vma=False
    )
```

```python
import jax
import jax.numpy as jnp
from jax import lax
from jax.sharding import Mesh, PartitionSpec as P

EX_DEV = 8
Z_HI, Y, CORE, Z_LO, X = 4, 8, 2, 3, 4
DP = ("zh", "y", "core")
MP = ("zl", "x")


def from_behind(array, axis, by):
    length = lax.axis_size(axis)
    return lax.ppermute(array, axis, [(i, (i + by) % length) for i in range(length)])


def block_features(token_factors, example_ids, left_factor, right_factor):
    proj_rank = left_factor.shape[1]
    tokens_here = token_factors.shape[1]
    examples = EX_DEV
    labels = example_ids[0]
    onehot = labels[:, None] == jnp.arange(examples, dtype=jnp.int32)[None, :]
    selector = onehot.astype(jnp.bfloat16)
    counts = jnp.sum(onehot.astype(jnp.float32), axis=0)
    inputs = token_factors[0, :, :proj_rank]
    outputs = token_factors[0, :, proj_rank:]
    masked = (selector[:, :, None] * inputs[:, None, :]).reshape(tokens_here, examples * proj_rank)
    summed = lax.dot_general(
        outputs, masked, (((0,), (0,)), ((), ())), preferred_element_type=jnp.float32
    )
    gradient = (
        summed.reshape(proj_rank, examples, proj_rank).transpose(1, 0, 2) / counts[:, None, None]
    )
    precond = jnp.einsum(
        "ac,ecd,db->eab",
        left_factor[0].astype(jnp.float32),
        gradient,
        right_factor[0].astype(jnp.float32),
        precision=lax.Precision.HIGHEST,
    )
    return precond.reshape(examples, proj_rank * proj_rank).astype(jnp.bfloat16)


def both_cores(mine, partner, core):
    return jnp.where(
        core == 0,
        jnp.concatenate([mine, partner], axis=0),
        jnp.concatenate([partner, mine], axis=0),
    )


def placing(width, position):
    source = lax.broadcasted_iota(jnp.int32, (width, width), 0)
    result = lax.broadcasted_iota(jnp.int32, (width, width), 1)
    example = source % EX_DEV
    z_hi = source // EX_DEV % Z_HI
    arrival = source // (EX_DEV * Z_HI) % Y
    core = source // (EX_DEV * Z_HI * Y)
    offset = jnp.where(arrival % 2 == 0, arrival // 2, Y - (arrival + 1) // 2)
    y = (position + offset) % Y
    return (result == ((z_hi * Y + y) * CORE + core) * EX_DEV + example).astype(jnp.float32)


def shards(token_factors, example_ids, left_factor, right_factor, query_features):
    rows = query_features.shape[0]
    features = block_features(token_factors, example_ids, left_factor, right_factor)
    partner = from_behind(query_features, "core", 1)
    queries = both_cores(query_features, partner, lax.axis_index("core"))

    copies = jnp.broadcast_to(features[None], (Z_HI,) + features.shape)
    column = lax.all_to_all(copies, "zh", 0, 0, tiled=False).reshape(Z_HI * EX_DEV, -1)

    up = down = column
    pieces = [column]
    for step in range(1, Y // 2):
        up = from_behind(up, "y", 1)
        down = from_behind(down, "y", -1)
        pieces += [up, down]
    half = column.shape[0] // 2
    pieces += [from_behind(up[:half], "y", 1), from_behind(down[half:], "y", -1)]

    scores = [
        lax.dot_general(
            queries, piece, (((1,), (1,)), ((), ())), preferred_element_type=jnp.float32
        ).astype(jnp.bfloat16)
        for piece in pieces
    ]
    members = Z_LO * X
    parts = jnp.concatenate(scores, axis=1).reshape(CORE * members, rows // members, -1)
    traded = lax.all_to_all(parts, ("core",) + MP, 0, 0, tiled=False)
    totals = jnp.sum(
        traded.astype(jnp.float32).reshape(CORE, members, rows // members, -1), axis=1
    )
    flat = jnp.concatenate([totals[0], totals[1]], axis=1)
    place = placing(flat.shape[1], lax.axis_index("y"))
    return lax.dot_general(
        flat,
        place,
        (((1,), (0,)), ((), ())),
        precision=lax.Precision.HIGHEST,
        preferred_element_type=jnp.float32,
    )


def solution(mesh):
    fine = Mesh(mesh.devices.reshape(Z_HI, Y, CORE, Z_LO, X), DP + MP)
    placed = (
        P(MP, DP, None),
        P(DP, None),
        P(MP, None, None),
        P(MP, None, None),
        P(DP, MP),
    )
    return jax.shard_map(
        shards, mesh=fine, in_specs=placed, out_specs=P(DP + MP, None), check_vma=False
    )
```

```python
import jax
import jax.numpy as jnp
from jax import lax
from jax.sharding import Mesh, PartitionSpec as P

EX_DEV = 8
Z_HI, Y, CORE, Z_LO, X = 4, 8, 2, 3, 4
DP = ("zh", "y", "core")
MP = ("zl", "x")


def from_behind(array, axis, by):
    length = lax.axis_size(axis)
    return lax.ppermute(array, axis, [(i, (i + by) % length) for i in range(length)])


def onward(array):
    steps = [
        ((i, core), ((i + (1 if core == 0 else Y - 1)) % Y, core)) for i in range(Y) for core in range(CORE)
    ]
    flat = [(a[0] * CORE + a[1], b[0] * CORE + b[1]) for a, b in steps]
    return lax.ppermute(array, ("y", "core"), flat)


def block_features(token_factors, example_ids, left_factor, right_factor):
    proj_rank = left_factor.shape[1]
    tokens_here = token_factors.shape[1]
    examples = EX_DEV
    labels = example_ids[0]
    onehot = labels[:, None] == jnp.arange(examples, dtype=jnp.int32)[None, :]
    selector = onehot.astype(jnp.bfloat16)
    counts = jnp.sum(onehot.astype(jnp.float32), axis=0)
    inputs = token_factors[0, :, :proj_rank]
    outputs = token_factors[0, :, proj_rank:]
    masked = (selector[:, :, None] * inputs[:, None, :]).reshape(tokens_here, examples * proj_rank)
    summed = lax.dot_general(
        outputs, masked, (((0,), (0,)), ((), ())), preferred_element_type=jnp.float32
    )
    gradient = (
        summed.reshape(proj_rank, examples, proj_rank).transpose(1, 0, 2) / counts[:, None, None]
    )
    precond = jnp.einsum(
        "ac,ecd,db->eab",
        left_factor[0].astype(jnp.float32),
        gradient,
        right_factor[0].astype(jnp.float32),
        precision=lax.Precision.HIGHEST,
    )
    return precond.reshape(examples, proj_rank * proj_rank).astype(jnp.bfloat16)


def both_cores(mine, partner, core):
    return jnp.where(
        core == 0,
        jnp.concatenate([mine, partner], axis=0),
        jnp.concatenate([partner, mine], axis=0),
    )


def placing(width, y):
    source = lax.broadcasted_iota(jnp.int32, (width, width), 0)
    result = lax.broadcasted_iota(jnp.int32, (width, width), 1)
    example = source % EX_DEV
    z_hi = source // EX_DEV % Z_HI
    piece = source // (EX_DEV * Z_HI) % Y
    core = source // (EX_DEV * Z_HI * Y)
    away = (piece + 1) // 2
    from_y = (y + jnp.where(core == 0, Y - away, away)) % Y
    from_core = jnp.where((piece % 2 == 1) | (piece == 0), core, 1 - core)
    return (result == ((z_hi * Y + from_y) * CORE + from_core) * EX_DEV + example).astype(
        jnp.bfloat16
    )


def to_all(array, axis):
    copies = jnp.broadcast_to(array[None], (lax.axis_size(axis),) + array.shape)
    return lax.all_to_all(copies, axis, 0, 0, tiled=False)


def scored(queries, pieces):
    return lax.dot_general(
        queries, pieces, (((1,), (1,)), ((), ())), preferred_element_type=jnp.float32
    )


def shards(token_factors, example_ids, left_factor, right_factor, query_features):
    rows, width = query_features.shape
    y, core = lax.axis_index("y"), lax.axis_index("core")
    features = block_features(token_factors, example_ids, left_factor, right_factor)
    features, query_features = lax.optimization_barrier((features, query_features))

    mine = to_all(features, "zh").reshape(Z_HI * EX_DEV, width)
    other = from_behind(query_features, "core", 1)
    queries = both_cores(query_features, other, core)
    place = placing(CORE * Y * Z_HI * EX_DEV, y)
    mine, place = lax.optimization_barrier((mine, place))

    partner = from_behind(mine, "core", 1)
    pieces = [mine]
    for step in range(1, Y // 2 + 1):
        mine = onward(mine)
        pieces.append(mine)
        if step < Y // 2:
            partner = onward(partner)
            pieces.append(partner)

    scores = [scored(queries, piece) for piece in pieces]
    members = Z_LO * X
    parts = jnp.concatenate([part.astype(jnp.bfloat16) for part in scores], axis=1)
    parts = parts.reshape(CORE * members, rows // members, -1)
    traded = lax.all_to_all(parts, ("core",) + MP, 0, 0, tiled=False).reshape(CORE, rows, -1)
    placed = sum(
        lax.dot_general(
            traded[i],
            place[i * traded.shape[2] : (i + 1) * traded.shape[2]],
            (((1,), (0,)), ((), ())),
            preferred_element_type=jnp.float32,
        )
        for i in range(CORE)
    )
    return jnp.sum(placed.reshape(members, rows // members, -1), axis=0)


def solution(mesh):
    fine = Mesh(mesh.devices.reshape(Z_HI, Y, CORE, Z_LO, X), DP + MP)
    placed = (
        P(MP, DP, None),
        P(DP, None),
        P(MP, None, None),
        P(MP, None, None),
        P(DP, MP),
    )
    return jax.shard_map(
        shards, mesh=fine, in_specs=placed, out_specs=P(DP + MP, None), check_vma=False
    )
```

```python
import jax
import jax.numpy as jnp
from jax import lax
from jax.experimental import pallas as pl
from jax.experimental.pallas import tpu as pltpu
from jax.sharding import Mesh, PartitionSpec as P

EX_DEV = 8
Z_HI, Y, CORE, Z_LO, X = 4, 8, 2, 3, 4
DP = ("zh", "y", "core")
MP = ("zl", "x")


def from_behind(array, axis, by):
    length = lax.axis_size(axis)
    return lax.ppermute(array, axis, [(i, (i + by) % length) for i in range(length)])


def onward(array):
    steps = [
        ((i, core), ((i + (1 if core == 0 else Y - 1)) % Y, core)) for i in range(Y) for core in range(CORE)
    ]
    flat = [(a[0] * CORE + a[1], b[0] * CORE + b[1]) for a, b in steps]
    return lax.ppermute(array, ("y", "core"), flat)


def thirds(array):
    first = array.astype(jnp.bfloat16)
    left = array - first.astype(jnp.float32)
    second = left.astype(jnp.bfloat16)
    third = (left - second.astype(jnp.float32)).astype(jnp.bfloat16)
    return first, second, third


def features_kernel(token_ref, label_ref, left_ref, right_ref, out_ref, found):
    rank = left_ref.shape[1]
    lanes = 2 * rank
    tokens = token_ref[0]
    members = lax.broadcasted_iota(jnp.int32, (EX_DEV, tokens.shape[0]), 0) == label_ref[...]
    chosen = members.astype(jnp.float32)
    counts = jnp.sum(chosen, axis=1, keepdims=True)
    chosen = chosen.astype(jnp.bfloat16)
    outputs = tokens.T[rank:]
    masked = jnp.concatenate([outputs * chosen[e : e + 1] for e in range(EX_DEV)], axis=0)
    summed = jnp.dot(masked, tokens, preferred_element_type=jnp.float32)
    gradient = jnp.concatenate(
        [summed[e * rank : (e + 1) * rank] / counts[e : e + 1] for e in range(EX_DEV)], axis=0
    )

    right = right_ref[0].astype(jnp.float32)
    right = jnp.concatenate([right, right], axis=1)
    right = jnp.concatenate([right, jnp.zeros_like(right)], axis=0).astype(jnp.bfloat16)
    turned = sum(
        jnp.dot(part, right, preferred_element_type=jnp.float32) for part in thirds(gradient)
    )

    group = 256
    left = left_ref[0].astype(jnp.float32)
    left = jnp.concatenate([left] * (group // rank), axis=1)
    left = jnp.concatenate([left] * (group // rank), axis=0)
    row = lax.broadcasted_iota(jnp.int32, (group, group), 0) // rank
    column = lax.broadcasted_iota(jnp.int32, (group, group), 1) // rank
    left = jnp.where(row == column, left, 0.0).astype(jnp.bfloat16)
    for start in range(0, EX_DEV * rank, group):
        parts = jnp.concatenate(thirds(turned[start : start + group]), axis=1)
        product = jnp.dot(left, parts, preferred_element_type=jnp.float32)
        found[start : start + group, :] = (
            product[:, :lanes] + product[:, lanes : 2 * lanes] + product[:, 2 * lanes :]
        )

    lane = lax.broadcasted_iota(jnp.int32, (EX_DEV, lanes), 1)
    for pair in range(rank // 2):
        even = found[pl.ds(2 * pair, EX_DEV, stride=rank), :]
        odd = found[pl.ds(2 * pair + 1, EX_DEV, stride=rank), :]
        tile = jnp.where(lane < rank, even, odd).astype(jnp.bfloat16)
        for copy in range(out_ref.shape[0]):
            out_ref[copy, :, pair * lanes : (pair + 1) * lanes] = tile


def block_features(token_factors, example_ids, left_factor, right_factor):
    rank = left_factor.shape[1]
    tokens = token_factors.shape[1]
    return pl.pallas_call(
        features_kernel,
        out_shape=jax.ShapeDtypeStruct((Z_HI, EX_DEV, rank * rank), jnp.bfloat16),
        scratch_shapes=[pltpu.VMEM((EX_DEV * rank, 2 * rank), jnp.float32)],
        cost_estimate=pl.CostEstimate(
            flops=2 * tokens * EX_DEV * rank * 2 * rank,
            bytes_accessed=tokens * rank * 4 + Z_HI * EX_DEV * rank * rank * 2,
            transcendentals=0,
        ),
        name="block_features",
    )(token_factors, example_ids, left_factor, right_factor)


def both_cores(mine, partner, core):
    return jnp.where(
        core == 0,
        jnp.concatenate([mine, partner], axis=0),
        jnp.concatenate([partner, mine], axis=0),
    )


def placing(width, y):
    source = lax.broadcasted_iota(jnp.int32, (width, width), 0)
    result = lax.broadcasted_iota(jnp.int32, (width, width), 1)
    example = source % EX_DEV
    z_hi = source // EX_DEV % Z_HI
    piece = source // (EX_DEV * Z_HI) % Y
    core = source // (EX_DEV * Z_HI * Y)
    away = (piece + 1) // 2
    from_y = (y + jnp.where(core == 0, Y - away, away)) % Y
    from_core = jnp.where((piece % 2 == 1) | (piece == 0), core, 1 - core)
    return (result == ((z_hi * Y + from_y) * CORE + from_core) * EX_DEV + example).astype(
        jnp.bfloat16
    )


def scored(queries, pieces):
    return lax.dot_general(
        queries, pieces, (((1,), (1,)), ((), ())), preferred_element_type=jnp.float32
    )


def shards(token_factors, example_ids, left_factor, right_factor, query_features):
    rows, width = query_features.shape
    y, core = lax.axis_index("y"), lax.axis_index("core")
    features = block_features(token_factors, example_ids, left_factor, right_factor)
    features, query_features = lax.optimization_barrier((features, query_features))

    mine = lax.all_to_all(features, "zh", 0, 0, tiled=False).reshape(Z_HI * EX_DEV, width)
    other = from_behind(query_features, "core", 1)
    queries = both_cores(query_features, other, core)
    place = placing(CORE * Y * Z_HI * EX_DEV, y)
    mine, place = lax.optimization_barrier((mine, place))

    partner = from_behind(mine, "core", 1)
    pieces = [mine]
    for step in range(1, Y // 2 + 1):
        mine = onward(mine)
        pieces.append(mine)
        if step < Y // 2:
            partner = onward(partner)
            pieces.append(partner)

    scores = [scored(queries, piece) for piece in pieces]
    members = Z_LO * X
    parts = jnp.concatenate([part.astype(jnp.bfloat16) for part in scores], axis=1)
    parts = parts.reshape(CORE * members, rows // members, -1)
    traded = lax.all_to_all(parts, ("core",) + MP, 0, 0, tiled=False).reshape(CORE, rows, -1)
    placed = sum(
        lax.dot_general(
            traded[i],
            place[i * traded.shape[2] : (i + 1) * traded.shape[2]],
            (((1,), (0,)), ((), ())),
            preferred_element_type=jnp.float32,
        )
        for i in range(CORE)
    )
    return jnp.sum(placed.reshape(members, rows // members, -1), axis=0)


def solution(mesh):
    fine = Mesh(mesh.devices.reshape(Z_HI, Y, CORE, Z_LO, X), DP + MP)
    placed = (
        P(MP, DP, None),
        P(DP, None),
        P(MP, None, None),
        P(MP, None, None),
        P(DP, MP),
    )
    return jax.shard_map(
        shards, mesh=fine, in_specs=placed, out_specs=P(DP + MP, None), check_vma=False
    )
```

```python
import jax
import jax.numpy as jnp
from jax import lax
from jax.experimental import pallas as pl
from jax.experimental.pallas import tpu as pltpu
from jax.sharding import Mesh, PartitionSpec as P

EX_DEV = 8
Z_HI, Y, CORE, Z_LO, X = 4, 8, 2, 3, 4
DP = ("zh", "y", "core")
MP = ("zl", "x")


def from_behind(array, axis, by):
    length = lax.axis_size(axis)
    return lax.ppermute(array, axis, [(i, (i + by) % length) for i in range(length)])


def onward(array, chips=1, swap=False):
    pairs = []
    for i in range(Y):
        for core in range(CORE):
            to = 1 - core if swap else core
            pairs.append((i * CORE + core, (i + (chips if to == 0 else -chips)) % Y * CORE + to))
    return lax.ppermute(array, ("y", "core"), pairs)


def thirds(array):
    first = array.astype(jnp.bfloat16)
    left = array - first.astype(jnp.float32)
    second = left.astype(jnp.bfloat16)
    third = (left - second.astype(jnp.float32)).astype(jnp.bfloat16)
    return first, second, third


def features_kernel(token_ref, label_ref, left_ref, right_ref, out_ref, found):
    rank = left_ref.shape[1]
    lanes = 2 * rank
    tokens = token_ref[0]
    members = lax.broadcasted_iota(jnp.int32, (EX_DEV, tokens.shape[0]), 0) == label_ref[...]
    chosen = members.astype(jnp.float32)
    counts = jnp.sum(chosen, axis=1, keepdims=True)
    chosen = chosen.astype(jnp.bfloat16)
    outputs = tokens.T[rank:]
    masked = jnp.concatenate([outputs * chosen[e : e + 1] for e in range(EX_DEV)], axis=0)
    summed = jnp.dot(masked, tokens, preferred_element_type=jnp.float32)
    gradient = jnp.concatenate(
        [summed[e * rank : (e + 1) * rank] / counts[e : e + 1] for e in range(EX_DEV)], axis=0
    )

    right = right_ref[0].astype(jnp.float32)
    right = jnp.concatenate([right, right], axis=1)
    right = jnp.concatenate([right, jnp.zeros_like(right)], axis=0).astype(jnp.bfloat16)
    turned = sum(
        jnp.dot(part, right, preferred_element_type=jnp.float32) for part in thirds(gradient)
    )

    group = 256
    left = left_ref[0].astype(jnp.float32)
    left = jnp.concatenate([left] * (group // rank), axis=1)
    left = jnp.concatenate([left] * (group // rank), axis=0)
    row = lax.broadcasted_iota(jnp.int32, (group, group), 0) // rank
    column = lax.broadcasted_iota(jnp.int32, (group, group), 1) // rank
    left = jnp.where(row == column, left, 0.0).astype(jnp.bfloat16)
    for start in range(0, EX_DEV * rank, group):
        parts = jnp.concatenate(thirds(turned[start : start + group]), axis=1)
        product = jnp.dot(left, parts, preferred_element_type=jnp.float32)
        found[start : start + group, :] = (
            product[:, :lanes] + product[:, lanes : 2 * lanes] + product[:, 2 * lanes :]
        )

    lane = lax.broadcasted_iota(jnp.int32, (EX_DEV, lanes), 1)
    for pair in range(rank // 2):
        even = found[pl.ds(2 * pair, EX_DEV, stride=rank), :]
        odd = found[pl.ds(2 * pair + 1, EX_DEV, stride=rank), :]
        tile = jnp.where(lane < rank, even, odd).astype(jnp.bfloat16)
        for copy in range(out_ref.shape[0]):
            out_ref[copy, :, pair * lanes : (pair + 1) * lanes] = tile


def block_features(token_factors, example_ids, left_factor, right_factor):
    rank = left_factor.shape[1]
    tokens = token_factors.shape[1]
    return pl.pallas_call(
        features_kernel,
        out_shape=jax.ShapeDtypeStruct((Z_HI, EX_DEV, rank * rank), jnp.bfloat16),
        scratch_shapes=[pltpu.VMEM((EX_DEV * rank, 2 * rank), jnp.float32)],
        cost_estimate=pl.CostEstimate(
            flops=2 * tokens * EX_DEV * rank * 2 * rank,
            bytes_accessed=tokens * rank * 4 + Z_HI * EX_DEV * rank * rank * 2,
            transcendentals=0,
        ),
        name="block_features",
    )(token_factors, example_ids, left_factor, right_factor)


def both_cores(mine, partner, core):
    return jnp.where(
        core == 0,
        jnp.concatenate([mine, partner], axis=0),
        jnp.concatenate([partner, mine], axis=0),
    )


def placing(width, y):
    source = lax.broadcasted_iota(jnp.int32, (width, width), 0)
    result = lax.broadcasted_iota(jnp.int32, (width, width), 1)
    example = source % EX_DEV
    z_hi = source // EX_DEV % Z_HI
    piece = source // (EX_DEV * Z_HI) % Y
    core = source // (EX_DEV * Z_HI * Y)
    away = (piece + 1) // 2
    from_y = (y + jnp.where(core == 0, Y - away, away)) % Y
    from_core = jnp.where((piece % 2 == 1) | (piece == 0), core, 1 - core)
    return (result == ((z_hi * Y + from_y) * CORE + from_core) * EX_DEV + example).astype(
        jnp.bfloat16
    )


def scored(queries, pieces):
    return lax.dot_general(
        queries, pieces, (((1,), (1,)), ((), ())), preferred_element_type=jnp.float32
    )


def shards(token_factors, example_ids, left_factor, right_factor, query_features):
    rows, width = query_features.shape
    y, core = lax.axis_index("y"), lax.axis_index("core")
    features = block_features(token_factors, example_ids, left_factor, right_factor)
    features, query_features = lax.optimization_barrier((features, query_features))

    mine = lax.all_to_all(features, "zh", 0, 0, tiled=False).reshape(Z_HI * EX_DEV, width)
    other = from_behind(query_features, "core", 1)
    queries = both_cores(query_features, other, core)
    place = placing(CORE * Y * Z_HI * EX_DEV, y)
    mine, place = lax.optimization_barrier((mine, place))

    near, cross = onward(mine), onward(mine, swap=True)
    pieces = [mine, near, cross]
    near, cross = onward(near), onward(cross)
    pieces += [near, cross]
    far = onward(near, chips=2)
    near, cross = onward(near), onward(cross)
    pieces += [near, cross, far]

    scores = [scored(queries, piece) for piece in pieces]
    members = Z_LO * X
    parts = jnp.concatenate([part.astype(jnp.bfloat16) for part in scores], axis=1)
    parts = parts.reshape(CORE * members, rows // members, -1)
    traded = lax.all_to_all(parts, ("core",) + MP, 0, 0, tiled=False).reshape(CORE, rows, -1)
    placed = sum(
        lax.dot_general(
            traded[i],
            place[i * traded.shape[2] : (i + 1) * traded.shape[2]],
            (((1,), (0,)), ((), ())),
            preferred_element_type=jnp.float32,
        )
        for i in range(CORE)
    )
    return jnp.sum(placed.reshape(members, rows // members, -1), axis=0)


def solution(mesh):
    fine = Mesh(mesh.devices.reshape(Z_HI, Y, CORE, Z_LO, X), DP + MP)
    placed = (
        P(MP, DP, None),
        P(DP, None),
        P(MP, None, None),
        P(MP, None, None),
        P(DP, MP),
    )
    return jax.shard_map(
        shards, mesh=fine, in_specs=placed, out_specs=P(DP + MP, None), check_vma=False
    )
```

```python
import jax
import jax.numpy as jnp
from jax import lax
from jax.experimental import pallas as pl
from jax.experimental.pallas import tpu as pltpu
from jax.sharding import Mesh, PartitionSpec as P

EX_DEV = 8
Z_HI, Y, CORE, Z_LO, X = 4, 8, 2, 3, 4
DP = ("zh", "y", "core")
MP = ("zl", "x")


def from_behind(array, axis, by):
    length = lax.axis_size(axis)
    return lax.ppermute(array, axis, [(i, (i + by) % length) for i in range(length)])


def onward(array, swap=False):
    pairs = []
    for i in range(Y):
        for core in range(CORE):
            to = 1 - core if swap else core
            pairs.append((i * CORE + core, (i + (1 if to == 0 else Y - 1)) % Y * CORE + to))
    return lax.ppermute(array, ("y", "core"), pairs)


def thirds(array):
    first = array.astype(jnp.bfloat16)
    left = array - first.astype(jnp.float32)
    second = left.astype(jnp.bfloat16)
    third = (left - second.astype(jnp.float32)).astype(jnp.bfloat16)
    return first, second, third


def features_kernel(token_ref, label_ref, left_ref, right_ref, out_ref, found):
    rank = left_ref.shape[1]
    lanes = 2 * rank
    tokens = token_ref[0]
    members = lax.broadcasted_iota(jnp.int32, (EX_DEV, tokens.shape[0]), 0) == label_ref[...]
    chosen = members.astype(jnp.float32)
    counts = jnp.sum(chosen, axis=1, keepdims=True)
    chosen = chosen.astype(jnp.bfloat16)
    outputs = tokens.T[rank:]
    masked = jnp.concatenate([outputs * chosen[e : e + 1] for e in range(EX_DEV)], axis=0)
    summed = jnp.dot(masked, tokens, preferred_element_type=jnp.float32)
    gradient = jnp.concatenate(
        [summed[e * rank : (e + 1) * rank] / counts[e : e + 1] for e in range(EX_DEV)], axis=0
    )

    right = right_ref[0].astype(jnp.float32)
    right = jnp.concatenate([right, right], axis=1)
    right = jnp.concatenate([right, jnp.zeros_like(right)], axis=0).astype(jnp.bfloat16)
    turned = sum(
        jnp.dot(part, right, preferred_element_type=jnp.float32) for part in thirds(gradient)
    )

    group = 256
    left = left_ref[0].astype(jnp.float32)
    left = jnp.concatenate([left] * (group // rank), axis=1)
    left = jnp.concatenate([left] * (group // rank), axis=0)
    row = lax.broadcasted_iota(jnp.int32, (group, group), 0) // rank
    column = lax.broadcasted_iota(jnp.int32, (group, group), 1) // rank
    left = jnp.where(row == column, left, 0.0).astype(jnp.bfloat16)
    for start in range(0, EX_DEV * rank, group):
        parts = jnp.concatenate(thirds(turned[start : start + group]), axis=1)
        product = jnp.dot(left, parts, preferred_element_type=jnp.float32)
        found[start : start + group, :] = (
            product[:, :lanes] + product[:, lanes : 2 * lanes] + product[:, 2 * lanes :]
        )

    lane = lax.broadcasted_iota(jnp.int32, (EX_DEV, lanes), 1)
    for pair in range(rank // 2):
        even = found[pl.ds(2 * pair, EX_DEV, stride=rank), :]
        odd = found[pl.ds(2 * pair + 1, EX_DEV, stride=rank), :]
        tile = jnp.where(lane < rank, even, odd).astype(jnp.bfloat16)
        for copy in range(out_ref.shape[0]):
            out_ref[copy, :, pair * lanes : (pair + 1) * lanes] = tile


def block_features(token_factors, example_ids, left_factor, right_factor):
    rank = left_factor.shape[1]
    tokens = token_factors.shape[1]
    return pl.pallas_call(
        features_kernel,
        out_shape=jax.ShapeDtypeStruct((Z_HI, EX_DEV, rank * rank), jnp.bfloat16),
        scratch_shapes=[pltpu.VMEM((EX_DEV * rank, 2 * rank), jnp.float32)],
        cost_estimate=pl.CostEstimate(
            flops=2 * tokens * EX_DEV * rank * 2 * rank,
            bytes_accessed=tokens * rank * 4 + Z_HI * EX_DEV * rank * rank * 2,
            transcendentals=0,
        ),
        name="block_features",
    )(token_factors, example_ids, left_factor, right_factor)


def both_cores(mine, partner, core):
    return jnp.where(
        core == 0,
        jnp.concatenate([mine, partner], axis=0),
        jnp.concatenate([partner, mine], axis=0),
    )


def placing(width, y):
    source = lax.broadcasted_iota(jnp.int32, (width, width), 0)
    result = lax.broadcasted_iota(jnp.int32, (width, width), 1)
    example = source % EX_DEV
    z_hi = source // EX_DEV % Z_HI
    piece = source // (EX_DEV * Z_HI) % Y
    core = source // (EX_DEV * Z_HI * Y)
    away = (piece + 1) // 2
    from_y = (y + jnp.where(core == 0, Y - away, away)) % Y
    from_core = jnp.where((piece % 2 == 1) | (piece == 0), core, 1 - core)
    return (result == ((z_hi * Y + from_y) * CORE + from_core) * EX_DEV + example).astype(
        jnp.bfloat16
    )


def scored(queries, pieces):
    return lax.dot_general(
        queries, pieces, (((1,), (1,)), ((), ())), preferred_element_type=jnp.float32
    )


def shards(token_factors, example_ids, left_factor, right_factor, query_features):
    rows, width = query_features.shape
    y, core = lax.axis_index("y"), lax.axis_index("core")
    features = block_features(token_factors, example_ids, left_factor, right_factor)
    features, query_features = lax.optimization_barrier((features, query_features))

    mine = lax.all_to_all(features, "zh", 0, 0, tiled=False).reshape(Z_HI * EX_DEV, width)
    other = from_behind(query_features, "core", 1)
    queries = both_cores(query_features, other, core)
    place = placing(CORE * Y * Z_HI * EX_DEV, y)
    mine, place = lax.optimization_barrier((mine, place))

    near, cross = onward(mine), onward(mine, swap=True)
    pieces = [mine, near, cross]
    for _ in (2, 3):
        near, cross = onward(near), onward(cross)
        pieces += [near, cross]
    pieces.append(onward(near))

    scores = [scored(queries, piece) for piece in pieces]
    members = Z_LO * X
    parts = jnp.concatenate([part.astype(jnp.bfloat16) for part in scores], axis=1)
    parts = parts.reshape(CORE * members, rows // members, -1)
    traded = lax.all_to_all(parts, ("core",) + MP, 0, 0, tiled=False).reshape(CORE, rows, -1)
    placed = sum(
        lax.dot_general(
            traded[i],
            place[i * traded.shape[2] : (i + 1) * traded.shape[2]],
            (((1,), (0,)), ((), ())),
            preferred_element_type=jnp.float32,
        )
        for i in range(CORE)
    )
    return jnp.sum(placed.reshape(members, rows // members, -1), axis=0)


def solution(mesh):
    fine = Mesh(mesh.devices.reshape(Z_HI, Y, CORE, Z_LO, X), DP + MP)
    placed = (
        P(MP, DP, None),
        P(DP, None),
        P(MP, None, None),
        P(MP, None, None),
        P(DP, MP),
    )
    return jax.shard_map(
        shards, mesh=fine, in_specs=placed, out_specs=P(DP + MP, None), check_vma=False
    )
```

```python
import jax
import jax.numpy as jnp
from jax import lax
from jax.experimental import pallas as pl
from jax.experimental.pallas import tpu as pltpu
from jax.sharding import Mesh, PartitionSpec as P

EX_DEV = 8
LOADS, STORES = 4, 2
Z_HI, Y, CORE, Z_LO, X = 4, 8, 2, 3, 4
DP = ("zh", "y", "core")
MP = ("zl", "x")


def from_behind(array, axis, by):
    length = lax.axis_size(axis)
    return lax.ppermute(array, axis, [(i, (i + by) % length) for i in range(length)])


def onward(array, swap=False):
    pairs = []
    for i in range(Y):
        for core in range(CORE):
            to = 1 - core if swap else core
            pairs.append((i * CORE + core, (i + (1 if to == 0 else Y - 1)) % Y * CORE + to))
    return lax.ppermute(array, ("y", "core"), pairs)


def thirds(array):
    first = array.astype(jnp.bfloat16)
    left = array - first.astype(jnp.float32)
    second = left.astype(jnp.bfloat16)
    third = (left - second.astype(jnp.float32)).astype(jnp.bfloat16)
    return first, second, third


def features_kernel(
    token_ref, label_ref, left_ref, right_ref, out_ref, held, found, made, load_sems, store_sems
):
    rank = left_ref.shape[1]
    lanes = 2 * rank
    tokens = held.shape[0] // LOADS

    def load(i):
        rows = pl.ds(i * tokens, tokens)
        return pltpu.make_async_copy(token_ref.at[0, rows, :], held.at[rows, :], load_sems.at[i])

    for i in range(LOADS):
        load(i).start()

    members = lax.broadcasted_iota(jnp.int32, (EX_DEV, held.shape[0]), 0) == label_ref[...]
    chosen = members.astype(jnp.float32)
    counts = jnp.sum(chosen, axis=1, keepdims=True)
    chosen = chosen.astype(jnp.bfloat16)

    right = right_ref[0].astype(jnp.float32)
    right = jnp.concatenate([right, right], axis=1)
    right = jnp.concatenate([right, jnp.zeros_like(right)], axis=0).astype(jnp.bfloat16)

    group = 256
    left = left_ref[0].astype(jnp.float32)
    left = jnp.concatenate([left] * (group // rank), axis=1)
    left = jnp.concatenate([left] * (group // rank), axis=0)
    row = lax.broadcasted_iota(jnp.int32, (group, group), 0) // rank
    column = lax.broadcasted_iota(jnp.int32, (group, group), 1) // rank
    left = jnp.where(row == column, left, 0.0).astype(jnp.bfloat16)

    summed = None
    for i in range(LOADS):
        load(i).wait()
        here = held[i * tokens : (i + 1) * tokens, :]
        outputs = here.T[rank:]
        picked = chosen[:, i * tokens : (i + 1) * tokens]
        masked = jnp.concatenate([outputs * picked[e : e + 1] for e in range(EX_DEV)], axis=0)
        product = jnp.dot(masked, here, preferred_element_type=jnp.float32)
        summed = product if summed is None else summed + product
    gradient = jnp.concatenate(
        [summed[e * rank : (e + 1) * rank] / counts[e : e + 1] for e in range(EX_DEV)], axis=0
    )
    turned = sum(
        jnp.dot(part, right, preferred_element_type=jnp.float32) for part in thirds(gradient)
    )
    for start in range(0, EX_DEV * rank, group):
        parts = jnp.concatenate(thirds(turned[start : start + group]), axis=1)
        product = jnp.dot(left, parts, preferred_element_type=jnp.float32)
        found[start : start + group, :] = (
            product[:, :lanes] + product[:, lanes : 2 * lanes] + product[:, 2 * lanes :]
        )

    def store(i, copy):
        columns = pl.ds(i * (made.shape[1] // STORES), made.shape[1] // STORES)
        return pltpu.make_async_copy(
            made.at[:, columns], out_ref.at[copy, :, columns], store_sems.at[i, copy]
        )

    lane = lax.broadcasted_iota(jnp.int32, (EX_DEV, lanes), 1)
    pairs = rank // 2 // STORES
    for i in range(STORES):
        for pair in range(i * pairs, (i + 1) * pairs):
            even = found[pl.ds(2 * pair, EX_DEV, stride=rank), :]
            odd = found[pl.ds(2 * pair + 1, EX_DEV, stride=rank), :]
            tile = jnp.where(lane < rank, even, odd).astype(jnp.bfloat16)
            made[:, pair * lanes : (pair + 1) * lanes] = tile
        for copy in range(Z_HI):
            store(i, copy).start()
    for i in range(STORES):
        for copy in range(Z_HI):
            store(i, copy).wait()


def block_features(token_factors, example_ids, left_factor, right_factor):
    rank = left_factor.shape[1]
    tokens = token_factors.shape[1]
    vmem = pl.BlockSpec(memory_space=pltpu.VMEM)
    return pl.pallas_call(
        features_kernel,
        out_shape=jax.ShapeDtypeStruct((Z_HI, EX_DEV, rank * rank), jnp.bfloat16),
        in_specs=[pl.BlockSpec(memory_space=pl.ANY), vmem, vmem, vmem],
        out_specs=pl.BlockSpec(memory_space=pl.ANY),
        scratch_shapes=[
            pltpu.VMEM((tokens, 2 * rank), jnp.bfloat16),
            pltpu.VMEM((EX_DEV * rank, 2 * rank), jnp.float32),
            pltpu.VMEM((EX_DEV, rank * rank), jnp.bfloat16),
            pltpu.SemaphoreType.DMA((LOADS,)),
            pltpu.SemaphoreType.DMA((STORES, Z_HI)),
        ],
        cost_estimate=pl.CostEstimate(
            flops=2 * tokens * EX_DEV * rank * 2 * rank,
            bytes_accessed=tokens * rank * 4 + Z_HI * EX_DEV * rank * rank * 2,
            transcendentals=0,
        ),
        name="block_features",
    )(token_factors, example_ids, left_factor, right_factor)


def both_cores(mine, partner, core):
    return jnp.where(
        core == 0,
        jnp.concatenate([mine, partner], axis=0),
        jnp.concatenate([partner, mine], axis=0),
    )


def placing(width, y):
    source = lax.broadcasted_iota(jnp.int32, (width, width), 0)
    result = lax.broadcasted_iota(jnp.int32, (width, width), 1)
    example = source % EX_DEV
    z_hi = source // EX_DEV % Z_HI
    piece = source // (EX_DEV * Z_HI) % Y
    core = source // (EX_DEV * Z_HI * Y)
    away = (piece + 1) // 2
    from_y = (y + jnp.where(core == 0, Y - away, away)) % Y
    from_core = jnp.where((piece % 2 == 1) | (piece == 0), core, 1 - core)
    return (result == ((z_hi * Y + from_y) * CORE + from_core) * EX_DEV + example).astype(
        jnp.bfloat16
    )


def scored(queries, pieces):
    return lax.dot_general(
        queries, pieces, (((1,), (1,)), ((), ())), preferred_element_type=jnp.float32
    )


def shards(token_factors, example_ids, left_factor, right_factor, query_features):
    rows, width = query_features.shape
    y, core = lax.axis_index("y"), lax.axis_index("core")
    features = block_features(token_factors, example_ids, left_factor, right_factor)
    features, query_features = lax.optimization_barrier((features, query_features))

    mine = lax.all_to_all(features, "zh", 0, 0, tiled=False).reshape(Z_HI * EX_DEV, width)
    other = from_behind(query_features, "core", 1)
    queries = both_cores(query_features, other, core)
    place = placing(CORE * Y * Z_HI * EX_DEV, y)
    mine, place = lax.optimization_barrier((mine, place))

    near, cross = onward(mine), onward(mine, swap=True)
    pieces = [mine, near, cross]
    for _ in (2, 3):
        near, cross = onward(near), onward(cross)
        pieces += [near, cross]
    pieces.append(onward(near))

    scores = [scored(queries, piece) for piece in pieces]
    members = Z_LO * X
    parts = jnp.concatenate([part.astype(jnp.bfloat16) for part in scores], axis=1)
    parts = parts.reshape(CORE * members, rows // members, -1)
    traded = lax.all_to_all(parts, ("core",) + MP, 0, 0, tiled=False).reshape(CORE, rows, -1)
    placed = lax.dot_general(
        jnp.concatenate([traded[i] for i in range(CORE)], axis=1),
        place,
        (((1,), (0,)), ((), ())),
        preferred_element_type=jnp.float32,
    )
    return jnp.sum(placed.reshape(members, rows // members, -1), axis=0)


def solution(mesh):
    fine = Mesh(mesh.devices.reshape(Z_HI, Y, CORE, Z_LO, X), DP + MP)
    placed = (
        P(MP, DP, None),
        P(DP, None),
        P(MP, None, None),
        P(MP, None, None),
        P(DP, MP),
    )
    return jax.shard_map(
        shards, mesh=fine, in_specs=placed, out_specs=P(DP + MP, None), check_vma=False
    )
```

```python
import jax
import jax.numpy as jnp
from jax import lax
from jax.experimental import pallas as pl
from jax.experimental.pallas import tpu as pltpu
from jax.sharding import Mesh, PartitionSpec as P

EX_DEV = 8
Z_HI, Y, CORE, Z_LO, X = 4, 8, 2, 3, 4
DP = ("zh", "y", "core")
MP = ("zl", "x")


def from_behind(array, axis, by):
    length = lax.axis_size(axis)
    return lax.ppermute(array, axis, [(i, (i + by) % length) for i in range(length)])


def onward(array, swap=False):
    pairs = []
    for i in range(Y):
        for core in range(CORE):
            to = 1 - core if swap else core
            pairs.append((i * CORE + core, (i + (1 if to == 0 else Y - 1)) % Y * CORE + to))
    return lax.ppermute(array, ("y", "core"), pairs)


def thirds(array):
    first = array.astype(jnp.bfloat16)
    left = array - first.astype(jnp.float32)
    second = left.astype(jnp.bfloat16)
    third = (left - second.astype(jnp.float32)).astype(jnp.bfloat16)
    return first, second, third


def features_kernel(token_ref, label_ref, left_ref, right_ref, out_ref, found):
    rank = left_ref.shape[1]
    lanes = 2 * rank
    tokens = token_ref[0]
    members = lax.broadcasted_iota(jnp.int32, (EX_DEV, tokens.shape[0]), 0) == label_ref[...]
    chosen = members.astype(jnp.float32)
    counts = jnp.sum(chosen, axis=1, keepdims=True)
    chosen = chosen.astype(jnp.bfloat16)
    outputs = tokens.T[rank:]
    masked = jnp.concatenate([outputs * chosen[e : e + 1] for e in range(EX_DEV)], axis=0)
    summed = jnp.dot(masked, tokens, preferred_element_type=jnp.float32)
    gradient = jnp.concatenate(
        [summed[e * rank : (e + 1) * rank] / counts[e : e + 1] for e in range(EX_DEV)], axis=0
    )

    right = right_ref[0].astype(jnp.float32)
    right = jnp.concatenate([right, right], axis=1)
    right = jnp.concatenate([right, jnp.zeros_like(right)], axis=0).astype(jnp.bfloat16)
    turned = sum(
        jnp.dot(part, right, preferred_element_type=jnp.float32) for part in thirds(gradient)
    )

    group = 256
    left = left_ref[0].astype(jnp.float32)
    left = jnp.concatenate([left] * (group // rank), axis=1)
    left = jnp.concatenate([left] * (group // rank), axis=0)
    row = lax.broadcasted_iota(jnp.int32, (group, group), 0) // rank
    column = lax.broadcasted_iota(jnp.int32, (group, group), 1) // rank
    left = jnp.where(row == column, left, 0.0).astype(jnp.bfloat16)
    for start in range(0, EX_DEV * rank, group):
        parts = jnp.concatenate(thirds(turned[start : start + group]), axis=1)
        product = jnp.dot(left, parts, preferred_element_type=jnp.float32)
        found[start : start + group, :] = (
            product[:, :lanes] + product[:, lanes : 2 * lanes] + product[:, 2 * lanes :]
        )

    lane = lax.broadcasted_iota(jnp.int32, (EX_DEV, lanes), 1)
    for pair in range(rank // 2):
        even = found[pl.ds(2 * pair, EX_DEV, stride=rank), :]
        odd = found[pl.ds(2 * pair + 1, EX_DEV, stride=rank), :]
        tile = jnp.where(lane < rank, even, odd).astype(jnp.bfloat16)
        for copy in range(out_ref.shape[0]):
            out_ref[copy, :, pair * lanes : (pair + 1) * lanes] = tile


def block_features(token_factors, example_ids, left_factor, right_factor):
    rank = left_factor.shape[1]
    tokens = token_factors.shape[1]
    return pl.pallas_call(
        features_kernel,
        out_shape=jax.ShapeDtypeStruct((Z_HI, EX_DEV, rank * rank), jnp.bfloat16),
        scratch_shapes=[pltpu.VMEM((EX_DEV * rank, 2 * rank), jnp.float32)],
        cost_estimate=pl.CostEstimate(
            flops=2 * tokens * EX_DEV * rank * 2 * rank,
            bytes_accessed=tokens * rank * 4 + Z_HI * EX_DEV * rank * rank * 2,
            transcendentals=0,
        ),
        name="block_features",
    )(token_factors, example_ids, left_factor, right_factor)


def both_cores(mine, partner, core):
    return jnp.where(
        core == 0,
        jnp.concatenate([mine, partner], axis=0),
        jnp.concatenate([partner, mine], axis=0),
    )


def placing(width, y):
    source = lax.broadcasted_iota(jnp.int32, (width, width), 0)
    result = lax.broadcasted_iota(jnp.int32, (width, width), 1)
    example = source % EX_DEV
    z_hi = source // EX_DEV % Z_HI
    piece = source // (EX_DEV * Z_HI) % Y
    core = source // (EX_DEV * Z_HI * Y)
    away = (piece + 1) // 2
    from_y = (y + jnp.where(core == 0, Y - away, away)) % Y
    from_core = jnp.where(piece % 2 == 0, core, 1 - core)
    return (result == ((z_hi * Y + from_y) * CORE + from_core) * EX_DEV + example).astype(
        jnp.bfloat16
    )


def scored(queries, pieces):
    return lax.dot_general(
        queries, pieces, (((1,), (1,)), ((), ())), preferred_element_type=jnp.float32
    )


def shards(token_factors, example_ids, left_factor, right_factor, query_features):
    rows, width = query_features.shape
    y, core = lax.axis_index("y"), lax.axis_index("core")
    features = block_features(token_factors, example_ids, left_factor, right_factor)
    features, query_features = lax.optimization_barrier((features, query_features))

    mine = lax.all_to_all(features, "zh", 0, 0, tiled=False).reshape(Z_HI * EX_DEV, width)
    other = from_behind(query_features, "core", 1)
    queries = both_cores(query_features, other, core)
    place = placing(CORE * Y * Z_HI * EX_DEV, y)
    mine, place = lax.optimization_barrier((mine, place))

    cross, near = onward(mine, swap=True), onward(mine)
    pieces = [mine, cross, near]
    for _ in (2, 3):
        cross, near = onward(cross), onward(near)
        pieces += [cross, near]
    pieces.append(onward(cross))

    scores = [scored(queries, piece) for piece in pieces]
    members = Z_LO * X
    parts = jnp.concatenate([part.astype(jnp.bfloat16) for part in scores], axis=1)
    parts = parts.reshape(CORE * members, rows // members, -1)
    traded = lax.all_to_all(parts, ("core",) + MP, 0, 0, tiled=False).reshape(CORE, rows, -1)
    placed = lax.dot_general(
        jnp.concatenate([traded[i] for i in range(CORE)], axis=1),
        place,
        (((1,), (0,)), ((), ())),
        preferred_element_type=jnp.float32,
    )
    return jnp.sum(placed.reshape(members, rows // members, -1), axis=0)


def solution(mesh):
    fine = Mesh(mesh.devices.reshape(Z_HI, Y, CORE, Z_LO, X), DP + MP)
    placed = (
        P(MP, DP, None),
        P(DP, None),
        P(MP, None, None),
        P(MP, None, None),
        P(DP, MP),
    )
    return jax.shard_map(
        shards, mesh=fine, in_specs=placed, out_specs=P(DP + MP, None), check_vma=False
    )
```
